512 devices in a mesh: pair: 16 (over z_hi, y), col: 32 (over x, z_lo, core).
Axes of the slice: x: 4, y: 8, z: 8 (z_hi: 2, z_lo: 4; z = z_hi * 4 + z_lo), core: 2. Of those that a mesh axis runs over, the one named last changes fastest.
Arguments:
- amplitudes: float32 [8192, 8192], P('pair', 'col'), may hold values from -6 to 6
- integrals: float32 [8192, 8192], P('pair', 'col'), may hold values from -0.125 to 0.125
- amp_tiles: int32 [16, 32, 4], P('pair', 'col'), may hold values from 0 to 7, as said below
- amp_count: int32 [16, 32], P('pair', 'col'), may hold values from 1 to 4, as said below
- int_mask: int32 [64, 64], P('pair', 'col'), may hold values 0 or 1
Outputs:
- ladder: float32 [8192, 8192], P('pair', 'col')
The draws below stay inside these ranges and needn't reach their ends.
Inputs may be any that keep to these rules, and one draw needn't show every extreme that they name: `amp_tiles`: in each device's list the entries are distinct tile numbers of that device's block. `amp_count`: some device's count equals 4 in every draw.
All inputs are finite; a program needn't handle non-finite values. No bound on the sum of `int_mask` on one device may be relied on, other than what follows from the above.
Results may differ from the reference program's by a relative error of at most 0.00007.
Values sent between devices are 32-bit elements; how exact they have to be, the bound alone decides.
No kernel may reach another device: no remote copies, remote signals or barrier semaphores. Data moves between devices by JAX's collectives and lax.ppermute only.
A program may use at most 128 MiB of HBM per device.

```python
import jax
import jax.numpy as jnp
from jax import lax

TILE = 128
PT_DEV = 4
KT_COL = 2
LIVE = 4
P_SIZE = 8192
K = 8192
N = 8192
KT = 64
NT = 64
N_PAIR = 16
N_COL = 32


def draw_amp_tiles(key, part):
    key_list = jax.random.split(key, N_PAIR * N_COL)

    def draw_one(subkey):
        return jax.random.permutation(subkey, PT_DEV * KT_COL)[:LIVE]
    chosen = jax.vmap(draw_one)(key_list)
    return chosen.astype(jnp.int32).reshape(N_PAIR, N_COL, LIVE)


def draw_amp_count(key, part):
    key_first, key_second = jax.random.split(key)
    counts = jax.random.randint(key_first, (N_PAIR * N_COL,), 1, LIVE + 1)
    full_at = jax.random.randint(key_second, (), 0, N_PAIR * N_COL)
    counts = jnp.where(jnp.arange(N_PAIR * N_COL) == full_at, LIVE, counts)
    return counts.reshape(N_PAIR, N_COL).astype(jnp.int32)


def set_ends(values, own_key, low, high):
    longest = values.shape.index(max(values.shape))
    spots = []
    for shift in (0, 1):
        where = [jax.random.randint(jax.random.fold_in(own_key, axis), (), 0, length) for axis, length in enumerate(values.shape)]
        where[longest] = (where[longest] + shift) % values.shape[longest]
        spots.append(tuple(where))
    return values.at[spots[0]].set(low).at[spots[1]].set(high)


def level_of(stream_key, dims, shards, smallest, largest):
    def one(axis_at, parts):
        draws = jax.random.uniform(jax.random.fold_in(jax.random.fold_in(stream_key, 6), axis_at), (parts,), jnp.float32, smallest / len(shards), largest / len(shards))
        return jnp.repeat(jnp.exp(draws), dims[axis_at] // parts).reshape((-1,) + (1,) * (len(dims) - axis_at - 1))

    level = one(*shards[0])
    for cut in shards[1:]:
        level = level * one(*cut)
    return level


def bell_draw(stream_key, extent, scale, bound, cuts=(), kind=jnp.bfloat16):
    drawn = scale * jax.random.normal(stream_key, extent, jnp.float32)
    if cuts:
        drawn = drawn * level_of(stream_key, extent, cuts, -0.22, 0.18)
    return jnp.clip(drawn, -bound, bound).astype(kind)


def setup_inputs(seed: int = 0) -> dict:
    keys = jax.random.split(jax.random.key(seed), 6)
    return {
        "amplitudes": bell_draw(keys[0], (P_SIZE, K), 1.0, 6.0, ((0, 16), (1, 32)), jnp.float32),
        "integrals": bell_draw(keys[1], (K, N), (K // 4) ** -0.5, 0.125, ((0, 16), (1, 32)), jnp.float32),
        "amp_tiles": draw_amp_tiles(jax.random.fold_in(keys[5], 71), 0),
        "amp_count": draw_amp_count(jax.random.fold_in(keys[5], 71), 0),
        "int_mask": set_ends((jax.random.randint(keys[4], (KT, NT), 0, 2) < 1).astype(jnp.int32), jax.random.fold_in(keys[4], 1), 0, 1),
    }


def expand_tiles(tile_mask):
    row_tiles = tile_mask.shape[0]
    col_tiles = tile_mask.shape[1]
    widened = jnp.broadcast_to(tile_mask[:, None, :, None], (row_tiles, TILE, col_tiles, TILE))
    return widened.reshape(row_tiles * TILE, col_tiles * TILE)


def occupancy(amp_tiles, amp_count):
    slot_index = jnp.arange(LIVE, dtype=jnp.int32)
    is_live = slot_index[None, None, :] < amp_count[:, :, None]
    tile_ids = jnp.arange(PT_DEV * KT_COL, dtype=jnp.int32)
    matches = (amp_tiles[:, :, :, None] == tile_ids[None, None, None, :]) & is_live[:, :, :, None]
    occupied = jnp.max(matches.astype(jnp.float32), axis=2)
    occupied = occupied.reshape(N_PAIR, N_COL, PT_DEV, KT_COL).transpose(0, 2, 1, 3)
    return occupied.reshape(N_PAIR * PT_DEV, N_COL * KT_COL)


def reference(amplitudes, integrals, amp_tiles, amp_count, int_mask):
    amp_sparse = amplitudes * expand_tiles(occupancy(amp_tiles, amp_count))
    int_sparse = integrals * expand_tiles(int_mask.astype(jnp.float32))
    return jnp.dot(amp_sparse, int_sparse, precision=lax.Precision.HIGHEST, preferred_element_type=jnp.float32)
```

```python
import jax
import jax.numpy as jnp
from jax import lax
from jax.experimental import pallas as pl
from jax.experimental.pallas import tpu as pltpu
from jax.sharding import PartitionSpec as P

TILE = 128
ZH, NY, NX, ZL, NC = 2, 8, 4, 4, 2
AXES = ("pair", "col")
F32 = jnp.float32
BF16 = jnp.bfloat16


def hop(value, move):
    def line(zh, y, x, zl, c):
        return (zh * NY + y) * (NX * ZL * NC) + (x * ZL + zl) * NC + c

    pairs = []
    for zh in range(ZH):
        for y in range(NY):
            for x in range(NX):
                for zl in range(ZL):
                    for c in range(NC):
                        there = move(zh, y, x, zl, c)
                        pairs.append((line(zh, y, x, zl, c), line(*there)))
    return lax.ppermute(value, AXES, pairs)


def swap_core(value):
    return hop(value, lambda zh, y, x, zl, c: (zh, y, x, zl, 1 - c))


def swap_half(value):
    return hop(value, lambda zh, y, x, zl, c: (1 - zh, y, x, zl, c))


def ring_y(value):
    return hop(value, lambda zh, y, x, zl, c: (zh, (y + 1 - 2 * c) % NY, x, zl, c))


def pack_kernel(tiles, count, amp, out):
    for s in range(4):
        t = tiles[0, 0, s]
        row = pl.multiple_of(lax.div(t, 2) * TILE, TILE)
        col = pl.multiple_of(lax.rem(t, 2) * TILE, TILE)
        out[s * TILE:(s + 1) * TILE, :] = amp[pl.ds(row, TILE), pl.ds(col, TILE)]
    slot = lax.broadcasted_iota(jnp.int32, (8, TILE), 0)
    ids = jnp.full((8, TILE), -1, jnp.int32)
    for s in range(4):
        ids = jnp.where((slot == s) & (s < count[0, 0]), tiles[0, 0, s], ids)
    out[4 * TILE:4 * TILE + 8, :] = ids.astype(F32)


def pack(amplitudes, tiles, count):
    return pl.pallas_call(
        pack_kernel,
        out_shape=jax.ShapeDtypeStruct((4 * TILE + 8, TILE), F32),
        in_specs=[
            pl.BlockSpec(memory_space=pltpu.SMEM),
            pl.BlockSpec(memory_space=pltpu.SMEM),
            pl.BlockSpec(memory_space=pltpu.VMEM),
        ],
        out_specs=pl.BlockSpec(memory_space=pltpu.VMEM),
        name="pack",
    )(tiles, count, amplitudes)


def mask_kernel(mask, src, out):
    for r in range(4):
        for k in range(2):
            at = (pl.ds(r * TILE, TILE), pl.ds(k * TILE, TILE))
            out[at] = src[at] * mask[r, k].astype(F32)


def mask_tiles(integrals, mask):
    return pl.pallas_call(
        mask_kernel,
        out_shape=jax.ShapeDtypeStruct(integrals.shape, F32),
        in_specs=[pl.BlockSpec(memory_space=pltpu.SMEM), pl.BlockSpec(memory_space=pltpu.VMEM)],
        out_specs=pl.BlockSpec(memory_space=pltpu.VMEM),
        name="mask",
    )(mask, integrals)


def split(value):
    high = value.astype(BF16)
    return high, (value - high.astype(F32)).astype(BF16)


def mm_kernel(units, first, *refs):
    if first:
        _, msg, b, out, a_hi, a_lo = refs
    else:
        _, msg, b, acc, out, a_hi, a_lo = refs
    for u in range(units):
        ids = [msg[u, 4 * TILE + s:4 * TILE + s + 1, :] for s in range(4)]
        for r in range(4):
            for k in range(2):
                t = float(r * 2 + k)
                tile = jnp.zeros((TILE, TILE), F32)
                for s in range(4):
                    tile = jnp.where(ids[s] == t, msg[u, s * TILE:(s + 1) * TILE, :], tile)
                high, low = split(tile)
                at = (pl.ds(r * TILE, TILE), pl.ds((u * 2 + k) * TILE, TILE))
                a_hi[at] = high
                a_lo[at] = low
    for n in range(2):
        b_hi, b_lo = split(b[n])
        total = jnp.dot(a_hi[...], b_hi, preferred_element_type=F32)
        total += jnp.dot(a_hi[...], b_lo, preferred_element_type=F32)
        total += jnp.dot(a_lo[...], b_hi, preferred_element_type=F32)
        out[n] = total if first else acc[n] + total


def mm(acc, gathered, b, index, units):
    depth = units * 2 * TILE
    first = acc is None
    shape = (2, 4 * TILE, 2 * TILE)
    whole = pl.BlockSpec(shape, lambda i, ix: (0, 0, 0))
    in_specs = [
        pl.BlockSpec((units, 4 * TILE + 8, TILE), lambda i, ix: (ix[0], 0, 0)),
        pl.BlockSpec((2, depth, 2 * TILE), lambda i, ix: (0, 0, 0)),
    ]
    args = [index.reshape(1), gathered, b]
    if not first:
        in_specs.append(whole)
        args.append(acc)

    def body(*refs):
        mm_kernel(units, first, *refs)

    return pl.pallas_call(
        body,
        out_shape=jax.ShapeDtypeStruct(shape, F32),
        grid_spec=pltpu.PrefetchScalarGridSpec(
            num_scalar_prefetch=1,
            grid=(1,),
            in_specs=in_specs,
            out_specs=whole,
            scratch_shapes=[pltpu.VMEM((4 * TILE, depth), BF16)] * 2,
        ),
        input_output_aliases={} if first else {3: 0},
        cost_estimate=pl.CostEstimate(
            flops=6 * 512 * 512 * depth, bytes_accessed=4000000, transcendentals=0
        ),
        name="mm",
    )(*args)


def local(amplitudes, integrals, amp_tiles, amp_count, int_mask):
    pair = lax.axis_index("pair")
    zh = lax.div(pair, NY)
    y = lax.rem(pair, NY)
    core = lax.rem(lax.axis_index("col"), NC)

    own = mask_tiles(integrals, int_mask)
    packed = pack(amplitudes, amp_tiles, amp_count)
    gathered = lax.all_gather(packed, "col", axis=0, tiled=False)

    other = swap_half(own)
    streams = [jnp.stack([own, swap_core(own)]), jnp.stack([other, swap_core(other)])]

    def half(block):
        return lax.dynamic_slice_in_dim(block, core * 2 * TILE, 2 * TILE, axis=1)

    away = jnp.where(core == 0, NY - 1, 1)
    work = []
    for i in range(2):
        side = zh if i == 0 else 1 - zh
        block = streams[i]
        work.append((0 + i, half(block), 2 * (side * NY + y) + core, 1))
        for s in range(1, 4):
            block = ring_y(block)
            work.append((2 * s + 3 * i, block, side * NY + lax.rem(y + s * away, NY), 2))
        block = ring_y(half(block))
        work.append((8 + 3 * i, block, 2 * (side * NY + lax.rem(y + 4, NY)) + core, 1))

    acc = None
    for _, block, index, units in sorted(work, key=lambda w: w[0]):
        acc = mm(acc, gathered, block, index, units)
    return acc[0] + swap_core(acc[1])


def solution(mesh):
    return jax.shard_map(
        local,
        mesh=mesh,
        in_specs=(
            P("pair", "col"),
            P("pair", "col"),
            P("pair", "col", None),
            P("pair", "col"),
            P("pair", "col"),
        ),
        out_specs=P("pair", "col"),
        check_vma=False,
    )
```

```python
import jax
import jax.numpy as jnp
from jax import lax
from jax.experimental import pallas as pl
from jax.experimental.pallas import tpu as pltpu
from jax.sharding import PartitionSpec as P


TILE = 128
ZH, NY, NX, ZL, NC = 2, 8, 4, 4, 2
AXES = ("pair", "col")
F32 = jnp.float32
BF16 = jnp.bfloat16


def hop(value, move):
    def line(zh, y, x, zl, c):
        return (zh * NY + y) * (NX * ZL * NC) + (x * ZL + zl) * NC + c

    pairs = []
    for zh in range(ZH):
        for y in range(NY):
            for x in range(NX):
                for zl in range(ZL):
                    for c in range(NC):
                        there = move(zh, y, x, zl, c)
                        if there is not None:
                            pairs.append((line(zh, y, x, zl, c), line(*there)))
    return lax.ppermute(value, AXES, pairs)


def swap_core(value):
    return hop(value, lambda zh, y, x, zl, c: (zh, y, x, zl, 1 - c))


def swap_half(value):
    return hop(value, lambda zh, y, x, zl, c: (1 - zh, y, x, zl, c))


def ring_y(value, cores=(0, 1)):
    return hop(
        value, lambda zh, y, x, zl, c: (zh, (y + 1 - 2 * c) % NY, x, zl, c) if c in cores else None
    )


def ring_x(value):
    return hop(value, lambda zh, y, x, zl, c: (zh, y, (x + 1 - 2 * c) % NX, zl, c))


def swap_run(value, bit):
    return hop(value, lambda zh, y, x, zl, c: (zh, y, x, zl ^ bit, c))


def pack_kernel(tiles, count, amp, out):
    for s in range(4):
        t = tiles[0, 0, s]
        row = pl.multiple_of(lax.div(t, 2) * TILE, TILE)
        col = pl.multiple_of(lax.rem(t, 2) * TILE, TILE)
        out[s * TILE:(s + 1) * TILE, :] = amp[pl.ds(row, TILE), pl.ds(col, TILE)]
    slot = lax.broadcasted_iota(jnp.int32, (8, TILE), 0)
    ids = jnp.full((8, TILE), -1, jnp.int32)
    for s in range(4):
        ids = jnp.where((slot == s) & (s < count[0, 0]), tiles[0, 0, s], ids)
    out[4 * TILE:4 * TILE + 8, :] = ids.astype(F32)


def pack(amplitudes, tiles, count):
    return pl.pallas_call(
        pack_kernel,
        out_shape=jax.ShapeDtypeStruct((4 * TILE + 8, TILE), F32),
        in_specs=[
            pl.BlockSpec(memory_space=pltpu.SMEM),
            pl.BlockSpec(memory_space=pltpu.SMEM),
            pl.BlockSpec(memory_space=pltpu.VMEM),
        ],
        out_specs=pl.BlockSpec(memory_space=pltpu.VMEM),
        compiler_params=pltpu.CompilerParams(vmem_limit_bytes=4 * 2**20),
        name="pack",
    )(tiles, count, amplitudes)


def mask_kernel(mask, src, out):
    for r in range(4):
        for k in range(2):
            at = (pl.ds(r * TILE, TILE), pl.ds(k * TILE, TILE))
            out[at] = src[at] * mask[k, r].astype(F32)


def mask_tiles(integrals, mask):
    return pl.pallas_call(
        mask_kernel,
        out_shape=jax.ShapeDtypeStruct(integrals.shape, F32),
        in_specs=[pl.BlockSpec(memory_space=pltpu.SMEM), pl.BlockSpec(memory_space=pltpu.VMEM)],
        out_specs=pl.BlockSpec(memory_space=pltpu.VMEM),
        compiler_params=pltpu.CompilerParams(vmem_limit_bytes=4 * 2**20),
        name="mask",
    )(mask.T, integrals)


def split(value):
    high = value.astype(BF16)
    return high, (value - high.astype(F32)).astype(BF16)


ROWS = 4 * TILE + 8
HALF = 2 * TILE
WHOLE = 4 * TILE
SUM = jax.ShapeDtypeStruct((WHOLE, HALF), F32)
VMEM = pl.BlockSpec(memory_space=pltpu.VMEM)
HBM = pl.BlockSpec(memory_space=pltpu.HBM)


def unpack(msg, a_cat):
    for h in range(2):
        ids = [msg[h, WHOLE + s:WHOLE + s + 1, :] for s in range(4)]
        for r in range(4):
            for k in range(2):
                t = float(r * 2 + k)
                tile = jnp.zeros((TILE, TILE), F32)
                for s in range(4):
                    tile = jnp.where(ids[s] == t, msg[h, s * TILE:(s + 1) * TILE, :], tile)
                high, low = split(tile)
                rows = pl.ds(r * TILE, TILE)
                a_cat[rows, pl.ds(h * HALF + k * TILE, TILE)] = high
                a_cat[rows, pl.ds(WHOLE + h * HALF + k * TILE, TILE)] = high
                a_cat[rows, pl.ds(2 * WHOLE + h * HALF + k * TILE, TILE)] = low


def product(a_cat, block):
    high, low = split(block)
    return jnp.dot(
        a_cat, jnp.concatenate([high, low, high]), preferred_element_type=F32
    )


def mm_kernel(n_sets, forms, first, ahead, table, *refs):
    n_blocks = len(forms)
    sets = [refs[4 * i:4 * i + 4] for i in range(n_sets)]
    refs = refs[4 * n_sets:]
    blocks = []
    for form in forms:
        blocks.append([refs[0].at[0], refs[0].at[1]] if form == 1 else list(refs[:2]))
        refs = refs[form:]
    if not first:
        olds, refs = refs[:2], refs[2:]
    sums, refs = refs[:2], refs[2:]
    if ahead:
        later, refs = refs[0], refs[1:]
    msg, rhs, a_cat, sems = refs

    for i in range(n_blocks + ahead):
        for h in range(2):
            for g in range(n_sets):
                for f in range(4):
                    @pl.when(table[h, i] == 4 * g + f)
                    def _():
                        source = sets[g][f].at[table[2 + h, i]]
                        pltpu.make_async_copy(source, msg.at[i, h], sems.at[h, i]).start()

        if i < n_blocks:
            @pl.when(table[0, i] >= 0)
            def _():
                for n in range(2):
                    source = blocks[i][n]
                    pltpu.make_async_copy(source, rhs.at[i, n], sems.at[2 + n, i]).start()

    for n in range(2):
        sums[n][...] = jnp.zeros((WHOLE, HALF), F32) if first else olds[n][...]

    def arrive(i):
        for h in range(2):
            pltpu.make_async_copy(sets[0][0].at[0], msg.at[i, h], sems.at[h, i]).wait()

    def body(i, carry):
        @pl.when(table[0, i] >= 0)
        def _():
            arrive(i)
            unpack(msg.at[i], a_cat)
            for n in range(2):
                pltpu.make_async_copy(blocks[0][0], rhs.at[i, n], sems.at[2 + n, i]).wait()
            for n in range(2):
                sums[n][...] += product(a_cat[...], rhs[i, n])

        return carry

    lax.fori_loop(0, n_blocks, body, 0)

    if ahead:
        @pl.when(table[0, n_blocks] >= 0)
        def _():
            arrive(n_blocks)
            unpack(msg.at[n_blocks], later)

        @pl.when(table[0, n_blocks] < 0)
        def _():
            later[...] = jnp.zeros((WHOLE, 3 * WHOLE), BF16)


def mm(sums, sets, blocks, table, ahead=0):
    first = sums is None
    args = [table]
    for group in sets:
        args += list(group)
    for block in blocks:
        args += list(block)
    specs = [pl.BlockSpec(memory_space=pltpu.SMEM)] + [HBM] * (len(args) - 1)
    aliases = {}
    if not first:
        aliases = {len(args): 0, len(args) + 1: 1}
        args += list(sums)
        specs += [VMEM] * 2
    count = len(blocks) + ahead
    forms = [len(block) for block in blocks]

    def body(*refs):
        mm_kernel(len(sets), forms, first, ahead, *refs)

    return pl.pallas_call(
        body,
        out_shape=[SUM, SUM] + [jax.ShapeDtypeStruct((WHOLE, 3 * WHOLE), BF16)] * ahead,
        in_specs=specs,
        out_specs=[VMEM] * (2 + ahead),
        scratch_shapes=[
            pltpu.VMEM((count, 2, ROWS, TILE), F32),
            pltpu.VMEM((len(blocks), 2, WHOLE, HALF), F32),
            pltpu.VMEM((WHOLE, 3 * WHOLE), BF16),
            pltpu.SemaphoreType.DMA((4, count)),
        ],
        input_output_aliases=aliases,
        cost_estimate=pl.CostEstimate(
            flops=6 * WHOLE**3 * len(blocks), bytes_accessed=1600000 * count, transcendentals=0
        ),
        compiler_params=pltpu.CompilerParams(vmem_limit_bytes=24 * 2**20),
        name="mm",
    )(*args)


def last_kernel(a_cat, block, *refs):
    total = product(a_cat[...], block[...])
    for ref in refs[:-1]:
        total += ref[...]
    refs[-1][...] = total


def last(ready, block, *addends):
    return pl.pallas_call(
        last_kernel,
        out_shape=SUM,
        in_specs=[VMEM] * (2 + len(addends)),
        out_specs=VMEM,
        cost_estimate=pl.CostEstimate(
            flops=3 * WHOLE**3, bytes_accessed=4000000, transcendentals=0
        ),
        compiler_params=pltpu.CompilerParams(vmem_limit_bytes=8 * 2**20),
        name="last",
    )(ready, block, *addends)


def after(value, *others):
    return lax.optimization_barrier((value,) + others)[0]


def ladder(amplitudes, integrals, amp_tiles, amp_count, int_mask):
    pair = lax.axis_index("pair")
    col = lax.axis_index("col")
    zh, y = lax.div(pair, NY), lax.rem(pair, NY)
    x, zl, core = lax.div(col, ZL * NC), lax.rem(lax.div(col, NC), ZL), lax.rem(col, NC)

    own = mask_tiles(integrals, int_mask)
    packed = pack(amplitudes, amp_tiles, amp_count)

    def spread(mine):
        quad = jnp.concatenate([mine, swap_core(mine)])
        near = ring_x(quad)
        return [quad, near, ring_x(near), swap_core(near)]

    other = swap_half(own)
    own_far = swap_core(own)
    start = [ring_y(own), ring_y(own_far)]
    first = [(own, own_far), (jnp.stack(start),)]
    for s in range(2, 5):
        first.append((ring_y(first[-1][0], (0, 1) if s < 4 else (0,)),))
    second = [(jnp.stack([other, swap_core(other)]),)]
    for _ in range(1, 4):
        second.append((ring_y(second[-1][0]),))
    end_far = ring_y(second[3][0][1], (1,))
    end_own = ring_y(second[3][0][0], (1,))

    arrived = after(swap_run(packed, 2), start[0])
    mine = jnp.stack([packed, arrived])
    theirs = swap_run(mine, 1)
    sets = [spread(mine), spread(theirs)]

    away = jnp.where(core == 0, NY - 1, 1)

    def table(stream, s, groups):
        side = jnp.where(stream == 0, zh, 1 - zh)
        q_y = (y + s * away) & (NY - 1)
        x_q, zl_q = side * 2 + (q_y >> 2), q_y & 3
        bits = zl_q ^ zl
        group, member = bits & 1, bits >> 1
        dx = (x_q - x) & (NX - 1)
        near = jnp.where(core == 0, 3, 1)
        field = jnp.where(dx == 0, 0, jnp.where(dx == near, 1, jnp.where(dx == 2, 2, 3)))
        live = jnp.where(s == 4, core == stream, jnp.where(s == 0, core != stream, True))
        live &= ((groups >> group) & 1) == 1
        field = jnp.where(live, group * 4 + field, -1)
        places = [jnp.where((core == h) != (dx == (near + 2) & 3), 0, 2) + member for h in range(2)]
        return jnp.stack([field, field] + places).astype(jnp.int32)

    def step(sums, groups, wanted, ahead=()):
        rows = jnp.array(wanted + list(ahead), jnp.int32).T
        blocks = [(first, second)[stream][s] for stream, s, _ in wanted]
        return mm(sums, sets[:groups], blocks, table(*rows), len(ahead))

    early = [(0, 0), (1, 0), (0, 1), (0, 2), (0, 3)]
    late = [(0, 4), (1, 1), (1, 2)]
    sums = step(None, 1, [b + (1,) for b in early])
    sums = step(sums, 1, [b + (1,) for b in late])
    sums = step(sums, 2, [b + (2,) for b in early + late])
    own_sum, far_sum, ready = step(sums, 2, [(1, 3, 3)], [(1, 4, 3)])
    far_sum = last(ready, end_far, far_sum)
    sent = swap_core(far_sum)
    return last(ready, end_own, own_sum, sent)


def solution(mesh):
    return jax.shard_map(
        ladder,
        mesh=mesh,
        in_specs=(
            P("pair", "col"),
            P("pair", "col"),
            P("pair", "col", None),
            P("pair", "col"),
            P("pair", "col"),
        ),
        out_specs=P("pair", "col"),
        check_vma=False,
    )
```

```python
import jax
import jax.numpy as jnp
from jax import lax
from jax.experimental import pallas as pl
from jax.experimental.pallas import tpu as pltpu
from jax.sharding import PartitionSpec as P


TILE = 128
ZH, NY, NX, ZL, NC = 2, 8, 4, 4, 2
AXES = ("pair", "col")
F32 = jnp.float32
BF16 = jnp.bfloat16


def hop(value, move):
    def line(zh, y, x, zl, c):
        return (zh * NY + y) * (NX * ZL * NC) + (x * ZL + zl) * NC + c

    pairs = []
    for zh in range(ZH):
        for y in range(NY):
            for x in range(NX):
                for zl in range(ZL):
                    for c in range(NC):
                        there = move(zh, y, x, zl, c)
                        if there is not None:
                            pairs.append((line(zh, y, x, zl, c), line(*there)))
    return lax.ppermute(value, AXES, pairs)


def swap_core(value):
    return hop(value, lambda zh, y, x, zl, c: (zh, y, x, zl, 1 - c))


def swap_half(value):
    return hop(value, lambda zh, y, x, zl, c: (1 - zh, y, x, zl, c))


def ring_y(value, cores=(0, 1)):
    return hop(
        value, lambda zh, y, x, zl, c: (zh, (y + 1 - 2 * c) % NY, x, zl, c) if c in cores else None
    )


def ring_x(value):
    return hop(value, lambda zh, y, x, zl, c: (zh, y, (x + 1 - 2 * c) % NX, zl, c))


def swap_run(value, bit):
    return hop(value, lambda zh, y, x, zl, c: (zh, y, x, zl ^ bit, c))


def prepare_kernel(amp_hbm, int_hbm, tiles_hbm, count_hbm, mask_hbm, packed, masked, *scratch):
    amp, integrals, tiles, count, mask, sems = scratch
    pairs = (
        (tiles_hbm, tiles), (count_hbm, count), (amp_hbm, amp), (mask_hbm, mask), (int_hbm, integrals)
    )
    copies = [pltpu.make_async_copy(a, b, sems.at[i]) for i, (a, b) in enumerate(pairs)]
    for copy in copies:
        copy.start()
    for copy in copies[:3]:
        copy.wait()
    for s in range(4):
        t = tiles[0, 0, s]
        row = pl.multiple_of(lax.div(t, 2) * TILE, TILE)
        col = pl.multiple_of(lax.rem(t, 2) * TILE, TILE)
        packed[s * TILE:(s + 1) * TILE, :] = amp[pl.ds(row, TILE), pl.ds(col, TILE)]
    slot = lax.broadcasted_iota(jnp.int32, (8, TILE), 0)
    ids = jnp.full((8, TILE), -1, jnp.int32)
    for s in range(4):
        ids = jnp.where((slot == s) & (s < count[0, 0]), tiles[0, 0, s], ids)
    packed[4 * TILE:4 * TILE + 8, :] = ids.astype(F32)
    for copy in copies[3:]:
        copy.wait()
    for r in range(4):
        for k in range(2):
            at = (pl.ds(r * TILE, TILE), pl.ds(k * TILE, TILE))
            masked[at] = integrals[at] * mask[k, r].astype(F32)


def prepare(amplitudes, integrals, tiles, count, mask):
    mask = mask.T
    return pl.pallas_call(
        prepare_kernel,
        out_shape=[
            jax.ShapeDtypeStruct((4 * TILE + 8, TILE), F32),
            jax.ShapeDtypeStruct(integrals.shape, F32),
        ],
        in_specs=[pl.BlockSpec(memory_space=pltpu.HBM)] * 5,
        out_specs=[pl.BlockSpec(memory_space=pltpu.VMEM)] * 2,
        scratch_shapes=[
            pltpu.VMEM(amplitudes.shape, F32),
            pltpu.VMEM(integrals.shape, F32),
            pltpu.SMEM(tiles.shape, jnp.int32),
            pltpu.SMEM(count.shape, jnp.int32),
            pltpu.SMEM(mask.shape, jnp.int32),
            pltpu.SemaphoreType.DMA((5,)),
        ],
        compiler_params=pltpu.CompilerParams(vmem_limit_bytes=60 * 2**20),
        name="prepare",
    )(amplitudes, integrals, tiles, count, mask)


def split(value):
    high = value.astype(BF16)
    return high, (value - high.astype(F32)).astype(BF16)


ROWS = 4 * TILE + 8
HALF = 2 * TILE
WHOLE = 4 * TILE
SUM = jax.ShapeDtypeStruct((WHOLE, HALF), F32)
VMEM = pl.BlockSpec(memory_space=pltpu.VMEM)
HBM = pl.BlockSpec(memory_space=pltpu.HBM)


def unpack(msg, ids, a_cat):
    a_cat[...] = jnp.zeros((WHOLE, 2 * WHOLE), BF16)
    for h in range(2):
        for s in range(4):
            t = ids[h, s, 0].astype(jnp.int32)

            @pl.when(t >= 0)
            def _():
                high, low = split(msg[h, s * TILE:(s + 1) * TILE, :])
                rows = pl.ds(pl.multiple_of((t >> 1) * TILE, TILE), TILE)
                col = pl.multiple_of((t & 1) * TILE, TILE)
                a_cat[rows, pl.ds(h * HALF + col, TILE)] = high
                a_cat[rows, pl.ds(WHOLE + h * HALF + col, TILE)] = low


def product(a_cat, block):
    high, low = split(block)
    total = jnp.dot(a_cat[...], jnp.concatenate([high, high]), preferred_element_type=F32)
    return total + jnp.dot(a_cat[:, :WHOLE], low, preferred_element_type=F32)


def mm_kernel(uses, forms, first, ahead, table, *refs):
    n_blocks = len(forms)
    sources, refs = refs[:len(uses)], refs[len(uses):]
    blocks = []
    for form in forms:
        blocks.append([refs[0].at[0], refs[0].at[1]] if form == 1 else list(refs[:2]))
        refs = refs[form:]
    if not first:
        olds, refs = refs[:2], refs[2:]
    sums, refs = refs[:2], refs[2:]
    if ahead:
        later, refs = refs[0], refs[1:]
    msg, rhs, a_cat, ids, sems = refs

    for i in range(n_blocks + ahead):
        for source, use in zip(sources, uses):
            @pl.when(table[0, i] == use)
            def _():
                for h in range(2):
                    tile = source.at[table[1 + h, i]]
                    pltpu.make_async_copy(tile, msg.at[i, h], sems.at[h, i]).start()
                    names = tile.at[pl.ds(WHOLE, 8), :]
                    pltpu.make_async_copy(names, ids.at[i, h], sems.at[4 + h, i]).start()

        if i < n_blocks:
            @pl.when(table[0, i] >= 0)
            def _():
                for n in range(2):
                    source = blocks[i][n]
                    pltpu.make_async_copy(source, rhs.at[i, n], sems.at[2 + n, i]).start()

    for n in range(2):
        sums[n][...] = jnp.zeros((WHOLE, HALF), F32) if first else olds[n][...]

    def arrive(i):
        for h in range(2):
            pltpu.make_async_copy(sources[0].at[0], msg.at[i, h], sems.at[h, i]).wait()
            names = sources[0].at[0, pl.ds(WHOLE, 8), :]
            pltpu.make_async_copy(names, ids.at[i, h], sems.at[4 + h, i]).wait()

    def body(i, carry):
        @pl.when(table[0, i] >= 0)
        def _():
            arrive(i)
            unpack(msg.at[i], ids.at[i], a_cat)
            for n in range(2):
                pltpu.make_async_copy(blocks[0][0], rhs.at[i, n], sems.at[2 + n, i]).wait()
            for n in range(2):
                sums[n][...] += product(a_cat, rhs[i, n])

        return carry

    lax.fori_loop(0, n_blocks, body, 0)

    if ahead:
        @pl.when(table[0, n_blocks] >= 0)
        def _():
            arrive(n_blocks)
            unpack(msg.at[n_blocks], ids.at[n_blocks], later)

        @pl.when(table[0, n_blocks] < 0)
        def _():
            later[...] = jnp.zeros((WHOLE, 2 * WHOLE), BF16)


def mm(sums, sets, uses, blocks, table, ahead=0):
    first = sums is None
    args = [table]
    args += [sets[use // 4][use % 4] for use in uses]
    for block in blocks:
        args += list(block)
    specs = [pl.BlockSpec(memory_space=pltpu.SMEM)] + [HBM] * (len(args) - 1)
    aliases = {}
    if not first:
        aliases = {len(args): 0, len(args) + 1: 1}
        args += list(sums)
        specs += [VMEM] * 2
    count = len(blocks) + ahead
    forms = [len(block) for block in blocks]

    def body(*refs):
        mm_kernel(uses, forms, first, ahead, *refs)

    return pl.pallas_call(
        body,
        out_shape=[SUM, SUM] + [jax.ShapeDtypeStruct((WHOLE, 2 * WHOLE), BF16)] * ahead,
        in_specs=specs,
        out_specs=[VMEM] * (2 + ahead),
        scratch_shapes=[
            pltpu.VMEM((count, 2, ROWS, TILE), F32),
            pltpu.VMEM((len(blocks), 2, WHOLE, HALF), F32),
            pltpu.VMEM((WHOLE, 2 * WHOLE), BF16),
            pltpu.SMEM((count, 2, 8, TILE), F32),
            pltpu.SemaphoreType.DMA((6, count)),
        ],
        input_output_aliases=aliases,
        cost_estimate=pl.CostEstimate(
            flops=6 * WHOLE**3 * len(blocks), bytes_accessed=1600000 * count, transcendentals=0
        ),
        compiler_params=pltpu.CompilerParams(vmem_limit_bytes=60 * 2**20),
        name="mm",
    )(*args)


def last_kernel(a_cat, block, *refs):
    total = product(a_cat, block[...])
    for ref in refs[:-1]:
        total += ref[...]
    refs[-1][...] = total


def last(ready, block, *addends):
    return pl.pallas_call(
        last_kernel,
        out_shape=SUM,
        in_specs=[VMEM] * (2 + len(addends)),
        out_specs=VMEM,
        cost_estimate=pl.CostEstimate(
            flops=3 * WHOLE**3, bytes_accessed=4000000, transcendentals=0
        ),
        compiler_params=pltpu.CompilerParams(vmem_limit_bytes=8 * 2**20),
        name="last",
    )(ready, block, *addends)


def ladder(amplitudes, integrals, amp_tiles, amp_count, int_mask):
    pair = lax.axis_index("pair")
    col = lax.axis_index("col")
    zh, y = lax.div(pair, NY), lax.rem(pair, NY)
    x, zl, core = lax.div(col, ZL * NC), lax.rem(lax.div(col, NC), ZL), lax.rem(col, NC)

    packed, own = prepare(amplitudes, integrals, amp_tiles, amp_count, int_mask)

    def spread(mine):
        quad = jnp.concatenate([mine, swap_core(mine)])
        near = ring_x(quad)
        return [quad, near, ring_x(near), swap_core(near)]

    other = swap_half(own)
    own_far = swap_core(own)
    start = [ring_y(own), ring_y(own_far)]
    first = [(own, own_far), (jnp.stack(start),)]
    for s in range(2, 5):
        first.append((ring_y(first[-1][0], (0, 1) if s < 4 else (0,)),))
    second = [(jnp.stack([other, swap_core(other)]),)]
    for _ in range(1, 4):
        second.append((ring_y(second[-1][0]),))
    end_far = ring_y(second[3][0][1], (1,))
    end_own = ring_y(second[3][0][0], (1,))

    arrived = swap_run(packed, 2)
    mine = jnp.stack([packed, arrived])
    theirs = swap_run(mine, 1)
    sets = [spread(mine), spread(theirs)]

    away = jnp.where(core == 0, NY - 1, 1)

    def table(stream, s, parts):
        side = jnp.where(stream == 0, zh, 1 - zh)
        q_y = (y + s * away) & (NY - 1)
        x_q, zl_q = side * 2 + (q_y >> 2), q_y & 3
        bits = zl_q ^ zl
        group, member = bits & 1, bits >> 1
        dx = (x_q - x) & (NX - 1)
        near = jnp.where(core == 0, 3, 1)
        field = jnp.where(dx == 0, 0, jnp.where(dx == near, 1, jnp.where(dx == 2, 2, 3)))
        live = jnp.where(s == 4, core == stream, jnp.where(s == 0, core != stream, True))
        live &= ((parts >> jnp.where(group == 0, 0, jnp.where(field == 2, 2, 1))) & 1) == 1
        field = jnp.where(live, group * 4 + field, -1)
        places = [jnp.where((core == h) != (dx == (near + 2) & 3), 0, 2) + member for h in range(2)]
        return jnp.stack([field] + places).astype(jnp.int32)

    def step(sums, uses, wanted, ahead=()):
        rows = jnp.array(wanted + list(ahead), jnp.int32).T
        blocks = [(first, second)[stream][s] for stream, s, _ in wanted]
        return mm(sums, sets, uses, blocks, table(*rows), len(ahead))

    early = [(0, 0), (1, 0), (0, 1), (0, 2), (0, 3)]
    late = [(0, 4), (1, 1), (1, 2)]
    sums = step(None, (0, 1, 2, 3), [b + (1,) for b in early])
    sums = step(sums, (0, 1, 2, 3, 4, 5, 7), [b + (2,) for b in early] + [b + (3,) for b in late])
    own_sum, far_sum, ready = step(
        sums, tuple(range(8)), [b + (4,) for b in early + late] + [(1, 3, 7)], [(1, 4, 7)]
    )
    far_sum = last(ready, end_far, far_sum)
    sent = swap_core(far_sum)
    return last(ready, end_own, own_sum, sent)


def solution(mesh):
    return jax.shard_map(
        ladder,
        mesh=mesh,
        in_specs=(
            P("pair", "col"),
            P("pair", "col"),
            P("pair", "col", None),
            P("pair", "col"),
            P("pair", "col"),
        ),
        out_specs=P("pair", "col"),
        check_vma=False,
    )
```

```python
import jax
import jax.numpy as jnp
from jax import lax
from jax.experimental import pallas as pl
from jax.experimental.pallas import tpu as pltpu
from jax.sharding import PartitionSpec as P


TILE = 128
ZH, NY, NX, ZL, NC = 2, 8, 4, 4, 2
AXES = ("pair", "col")
F32 = jnp.float32
BF16 = jnp.bfloat16


def hop(value, move):
    def line(zh, y, x, zl, c):
        return (zh * NY + y) * (NX * ZL * NC) + (x * ZL + zl) * NC + c

    pairs = []
    for zh in range(ZH):
        for y in range(NY):
            for x in range(NX):
                for zl in range(ZL):
                    for c in range(NC):
                        there = move(zh, y, x, zl, c)
                        if there is not None:
                            pairs.append((line(zh, y, x, zl, c), line(*there)))
    return lax.ppermute(value, AXES, pairs)


def swap_core(value):
    return hop(value, lambda zh, y, x, zl, c: (zh, y, x, zl, 1 - c))


def swap_half(value):
    return hop(value, lambda zh, y, x, zl, c: (1 - zh, y, x, zl, c))


def ring_y(value, cores=(0, 1)):
    return hop(
        value, lambda zh, y, x, zl, c: (zh, (y + 1 - 2 * c) % NY, x, zl, c) if c in cores else None
    )


def ring_x(value):
    return hop(value, lambda zh, y, x, zl, c: (zh, y, (x + 1 - 2 * c) % NX, zl, c))


def swap_run(value, bit):
    return hop(value, lambda zh, y, x, zl, c: (zh, y, x, zl ^ bit, c))


def prepare_kernel(amp_hbm, int_hbm, tiles_hbm, count_hbm, mask_hbm, packed, masked, *scratch):
    amp, integrals, tiles, count, mask, sems = scratch
    pairs = (
        (tiles_hbm, tiles), (count_hbm, count), (amp_hbm, amp), (mask_hbm, mask), (int_hbm, integrals)
    )
    copies = [pltpu.make_async_copy(a, b, sems.at[i]) for i, (a, b) in enumerate(pairs)]
    for copy in copies:
        copy.start()
    for copy in copies[:3]:
        copy.wait()
    for s in range(4):
        t = tiles[0, 0, s]
        row = pl.multiple_of(lax.div(t, 2) * TILE, TILE)
        col = pl.multiple_of(lax.rem(t, 2) * TILE, TILE)
        packed[s * TILE:(s + 1) * TILE, :] = amp[pl.ds(row, TILE), pl.ds(col, TILE)]
    slot = lax.broadcasted_iota(jnp.int32, (8, TILE), 0)
    ids = jnp.full((8, TILE), -1, jnp.int32)
    for s in range(4):
        ids = jnp.where((slot == s) & (s < count[0, 0]), tiles[0, 0, s], ids)
    packed[4 * TILE:4 * TILE + 8, :] = ids.astype(F32)
    for copy in copies[3:]:
        copy.wait()
    for r in range(4):
        for k in range(2):
            at = (pl.ds(r * TILE, TILE), pl.ds(k * TILE, TILE))
            masked[at] = integrals[at] * mask[k, r].astype(F32)


def prepare(amplitudes, integrals, tiles, count, mask):
    mask = mask.T
    return pl.pallas_call(
        prepare_kernel,
        out_shape=[
            jax.ShapeDtypeStruct((4 * TILE + 8, TILE), F32),
            jax.ShapeDtypeStruct(integrals.shape, F32),
        ],
        in_specs=[pl.BlockSpec(memory_space=pltpu.HBM)] * 5,
        out_specs=[pl.BlockSpec(memory_space=pltpu.VMEM)] * 2,
        scratch_shapes=[
            pltpu.VMEM(amplitudes.shape, F32),
            pltpu.VMEM(integrals.shape, F32),
            pltpu.SMEM(tiles.shape, jnp.int32),
            pltpu.SMEM(count.shape, jnp.int32),
            pltpu.SMEM(mask.shape, jnp.int32),
            pltpu.SemaphoreType.DMA((5,)),
        ],
        compiler_params=pltpu.CompilerParams(vmem_limit_bytes=60 * 2**20),
        name="prepare",
    )(amplitudes, integrals, tiles, count, mask)


def split(value):
    high = value.astype(BF16)
    return high, (value - high.astype(F32)).astype(BF16)


ROWS = 4 * TILE + 8
HALF = 2 * TILE
WHOLE = 4 * TILE
SUM = jax.ShapeDtypeStruct((WHOLE, HALF), F32)
VMEM = pl.BlockSpec(memory_space=pltpu.VMEM)
HBM = pl.BlockSpec(memory_space=pltpu.HBM)


def unpack(msg, ids, a_cat):
    a_cat[...] = jnp.zeros((WHOLE, 2 * WHOLE), BF16)
    for h in range(2):
        for s in range(4):
            t = ids[h, s, 0].astype(jnp.int32)

            @pl.when(t >= 0)
            def _():
                high, low = split(msg[h, s * TILE:(s + 1) * TILE, :])
                rows = pl.ds(pl.multiple_of((t >> 1) * TILE, TILE), TILE)
                col = pl.multiple_of((t & 1) * TILE, TILE)
                a_cat[rows, pl.ds(h * HALF + col, TILE)] = high
                a_cat[rows, pl.ds(WHOLE + h * HALF + col, TILE)] = low


def product(a_cat, block):
    high, low = split(block)
    total = jnp.dot(a_cat[...], jnp.concatenate([high, high]), preferred_element_type=F32)
    return total + jnp.dot(a_cat[:, :WHOLE], low, preferred_element_type=F32)


def mm_kernel(uses, forms, first, ahead, base, rows, *refs):
    n_blocks = len(forms)
    sources, refs = refs[:len(uses)], refs[len(uses):]
    blocks = []
    for form in forms:
        blocks.append([refs[0].at[0], refs[0].at[1]] if form == 1 else list(refs[:2]))
        refs = refs[form:]
    if not first:
        olds, refs = refs[:2], refs[2:]
    sums, refs = refs[:2], refs[2:]
    if ahead:
        later, refs = refs[0], refs[1:]
    msg, rhs, a_cat, ids, sems = refs

    for i in range(n_blocks + ahead):
        for source, use in zip(sources, uses):
            @pl.when(rows[0, base + i] == use)
            def _():
                for h in range(2):
                    tile = source.at[rows[1 + h, base + i]]
                    pltpu.make_async_copy(tile, msg.at[i, h], sems.at[h, i]).start()
                    names = tile.at[pl.ds(WHOLE, 8), :]
                    pltpu.make_async_copy(names, ids.at[i, h], sems.at[4 + h, i]).start()

        if i < n_blocks:
            @pl.when(rows[0, base + i] >= 0)
            def _():
                for n in range(2):
                    source = blocks[i][n]
                    pltpu.make_async_copy(source, rhs.at[i, n], sems.at[2 + n, i]).start()

    for n in range(2):
        sums[n][...] = jnp.zeros((WHOLE, HALF), F32) if first else olds[n][...]

    def arrive(i):
        for h in range(2):
            pltpu.make_async_copy(sources[0].at[0], msg.at[i, h], sems.at[h, i]).wait()
            names = sources[0].at[0, pl.ds(WHOLE, 8), :]
            pltpu.make_async_copy(names, ids.at[i, h], sems.at[4 + h, i]).wait()

    def body(i, carry):
        @pl.when(rows[0, base + i] >= 0)
        def _():
            arrive(i)
            unpack(msg.at[i], ids.at[i], a_cat)
            for n in range(2):
                pltpu.make_async_copy(blocks[0][0], rhs.at[i, n], sems.at[2 + n, i]).wait()
            for n in range(2):
                sums[n][...] += product(a_cat, rhs[i, n])

        return carry

    lax.fori_loop(0, n_blocks, body, 0)

    if ahead:
        @pl.when(rows[0, base + n_blocks] >= 0)
        def _():
            arrive(n_blocks)
            unpack(msg.at[n_blocks], ids.at[n_blocks], later)

        @pl.when(rows[0, base + n_blocks] < 0)
        def _():
            later[...] = jnp.zeros((WHOLE, 2 * WHOLE), BF16)


def mm(sums, sets, uses, blocks, rows, base, ahead):
    first = sums is None
    args = [rows]
    args += [sets[use // 4][use % 4] for use in uses]
    for block in blocks:
        args += list(block)
    specs = [pl.BlockSpec(memory_space=pltpu.SMEM)] + [HBM] * (len(args) - 1)
    aliases = {}
    if not first:
        aliases = {len(args): 0, len(args) + 1: 1}
        args += list(sums)
        specs += [VMEM] * 2
    count = len(blocks) + ahead
    forms = [len(block) for block in blocks]

    def body(*refs):
        mm_kernel(uses, forms, first, ahead, base, *refs)

    return pl.pallas_call(
        body,
        out_shape=[SUM, SUM] + [jax.ShapeDtypeStruct((WHOLE, 2 * WHOLE), BF16)] * ahead,
        in_specs=specs,
        out_specs=[VMEM] * (2 + ahead),
        scratch_shapes=[
            pltpu.VMEM((count, 2, ROWS, TILE), F32),
            pltpu.VMEM((len(blocks), 2, WHOLE, HALF), F32),
            pltpu.VMEM((WHOLE, 2 * WHOLE), BF16),
            pltpu.SMEM((count, 2, 8, TILE), F32),
            pltpu.SemaphoreType.DMA((6, count)),
        ],
        input_output_aliases=aliases,
        cost_estimate=pl.CostEstimate(
            flops=6 * WHOLE**3 * len(blocks), bytes_accessed=1600000 * count, transcendentals=0
        ),
        compiler_params=pltpu.CompilerParams(vmem_limit_bytes=60 * 2**20),
        name="mm",
    )(*args)


def last_kernel(a_cat, block, *refs):
    total = product(a_cat, block[...])
    for ref in refs[:-1]:
        total += ref[...]
    refs[-1][...] = total


def last(ready, block, *addends):
    return pl.pallas_call(
        last_kernel,
        out_shape=SUM,
        in_specs=[VMEM] * (2 + len(addends)),
        out_specs=VMEM,
        cost_estimate=pl.CostEstimate(
            flops=3 * WHOLE**3, bytes_accessed=4000000, transcendentals=0
        ),
        compiler_params=pltpu.CompilerParams(vmem_limit_bytes=8 * 2**20),
        name="last",
    )(ready, block, *addends)


def ladder(amplitudes, integrals, amp_tiles, amp_count, int_mask):
    pair = lax.axis_index("pair")
    col = lax.axis_index("col")
    zh, y = lax.div(pair, NY), lax.rem(pair, NY)
    x, zl, core = lax.div(col, ZL * NC), lax.rem(lax.div(col, NC), ZL), lax.rem(col, NC)

    packed, own = prepare(amplitudes, integrals, amp_tiles, amp_count, int_mask)

    def spread(mine):
        quad = jnp.concatenate([mine, swap_core(mine)])
        near = ring_x(quad)
        return [quad, near, ring_x(near), swap_core(near)]

    other = swap_half(own)
    own_far = swap_core(own)
    start = [ring_y(own), ring_y(own_far)]
    first = [(own, own_far), (jnp.stack(start),)]
    for s in range(2, 5):
        first.append((ring_y(first[-1][0], (0, 1) if s < 4 else (0,)),))
    second = [(jnp.stack([other, swap_core(other)]),)]
    for _ in range(1, 3):
        second.append((ring_y(second[-1][0]),))
    second.append(tuple(ring_y(second[2][0][n]) for n in range(2)))
    end_own = ring_y(second[3][0], (1,))
    end_far = ring_y(second[3][1], (1,))

    arrived = swap_run(packed, 2)
    mine = jnp.stack([packed, arrived])
    theirs = swap_run(mine, 1)
    sets = [spread(mine), spread(theirs)]

    away = jnp.where(core == 0, NY - 1, 1)

    def table(stream, s, parts):
        side = jnp.where(stream == 0, zh, 1 - zh)
        q_y = (y + s * away) & (NY - 1)
        x_q, zl_q = side * 2 + (q_y >> 2), q_y & 3
        bits = zl_q ^ zl
        group, member = bits & 1, bits >> 1
        dx = (x_q - x) & (NX - 1)
        near = jnp.where(core == 0, 3, 1)
        field = jnp.where(dx == 0, 0, jnp.where(dx == near, 1, jnp.where(dx == 2, 2, 3)))
        live = jnp.where(s == 4, core == stream, jnp.where(s == 0, core != stream, True))
        live &= ((parts >> jnp.where(group == 0, 0, jnp.where(field == 2, 2, 1))) & 1) == 1
        field = jnp.where(live, group * 4 + field, -1)
        places = [jnp.where((core == h) != (dx == (near + 2) & 3), 0, 2) + member for h in range(2)]
        return jnp.stack([field] + places).astype(jnp.int32)

    early = [(0, 0), (1, 0), (0, 1), (0, 2), (0, 3), (1, 1)]
    late = [(0, 4), (1, 2)]
    plans = {
        "mm_a": ((0, 1, 2, 3), [b + (1,) for b in early]),
        "mm_c": ((0, 1, 2, 3, 4, 5, 7), [b + (2,) for b in early] + [b + (3,) for b in late]),
        "mm_d": (tuple(range(8)), [b + (4,) for b in early + late] + [(1, 3, 7), (1, 4, 7)]),
    }
    rows = table(*jnp.array(sum((plan[1] for plan in plans.values()), []), jnp.int32).T)
    base, results = 0, None
    for name, (uses, wanted) in plans.items():
        ahead = int(name == "mm_d")
        blocks = [(first, second)[stream][s] for stream, s, _ in wanted[:len(wanted) - ahead]]
        results = mm(results, sets, uses, blocks, rows, base, ahead)
        base += len(wanted)
    own_sum, far_sum, ready = results
    far_sum = last(ready, end_far, far_sum)
    sent = swap_core(far_sum)
    return last(ready, end_own, own_sum, sent)


def solution(mesh):
    return jax.shard_map(
        ladder,
        mesh=mesh,
        in_specs=(
            P("pair", "col"),
            P("pair", "col"),
            P("pair", "col", None),
            P("pair", "col"),
            P("pair", "col"),
        ),
        out_specs=P("pair", "col"),
        check_vma=False,
    )
```
